32 devices in a mesh: mem: 8 (over z, y), lat: 4 (over x, core).
Axes of the slice: x: 2, y: 2, z: 4, core: 2. Of those that a mesh axis runs over, the one named last changes fastest.
Arguments:
- prior_state: bfloat16 [512, 64, 8, 128], P('mem', None, 'lat'), may hold values from -6 to 6
- norm_scale: float32 [64], replicated, may hold values from 0.1 to 1.9
- entry_kernel: bfloat16 [9, 256, 64], replicated, may hold values from -0.25 to 0.25
- closing_filter: bfloat16 [9, 64, 256], replicated, may hold values from -0.125 to 0.125
- observed_cell: int32 [8, 4, 16], P('mem', 'lat'), may hold values from 0 to 31
- observed_weight: float32 [8, 4, 16, 64], P('mem', 'lat'), may hold values from -0.75 to 0.75
- observed_value: float32 [8, 4, 16], P('mem', 'lat'), may hold values from -6 to 6
- observed_precision: float32 [8, 4, 16], P('mem', 'lat'), may hold values from 0.25 to 2
Outputs:
- analysed: float32 [128, 8, 64, 512], P('mem', 'lat')
The draws below stay inside these ranges and needn't reach their ends.
Inputs may be any that keep to these rules, and one draw needn't show every extreme that they name: observed_cell is (column within the 16 columns of its group) * 2 + (row within its band).
All inputs are finite; a program needn't handle non-finite values.
Results may differ from the reference program's by a relative error of at most 0.0036.
Values may be sent and summed in bfloat16 or wider, within the bound.
A program may use at most 128 MiB of HBM per device.

```python
import math
import jax
import jax.numpy as jnp
from jax import lax

ENSEMBLE_SIZE = 512
FIELD_NUMBER = 64
F = 256
ZONAL_POINTS = 128
STRIP_HEIGHT = 2
OBS_DEV = 16
NS_ITERS = 3
PARALLEL_STRIPS = 4
ZONAL_SECTORS = 8
MERIDIAN_POINTS = 8
SECTOR_WIDTH = 16
CELLS_REG = 32
REGION_ROWS = 2048


def set_ends(array, rng, smallest, top_value):
    longest = array.shape.index(max(array.shape))
    spots = []
    for shift in (0, 1):
        where = [jax.random.randint(jax.random.fold_in(rng, axis), (), 0, length) for axis, length in enumerate(array.shape)]
        where[longest] = (where[longest] + shift) % array.shape[longest]
        spots.append(tuple(where))
    return array.at[spots[0]].set(smallest).at[spots[1]].set(top_value)


def shard_levels(stream_key, shape, cuts, smallest, high):
    def one(position, shards_of):
        heights = jax.random.uniform(jax.random.fold_in(jax.random.fold_in(stream_key, 6), position), (shards_of,), jnp.float32, smallest / len(cuts), high / len(cuts))
        return jnp.repeat(jnp.exp(heights), shape[position] // shards_of).reshape((-1,) + (1,) * (len(shape) - position - 1))

    gain = one(*cuts[0])
    for cut in cuts[1:]:
        gain = gain * one(*cut)
    return gain


def gaussian(stream_key, shape, scale, most, shards=(), held_as=jnp.bfloat16):
    factor_of = shard_levels(stream_key, shape, shards, -0.22, 0.18) if shards else 1.0
    values = jax.random.normal(stream_key, shape, jnp.float32) * scale * factor_of
    return jnp.minimum(jnp.maximum(values, -most), most).astype(held_as)


def setup_inputs(seed: int = 0) -> dict:
    streams_of = jax.random.split(jax.random.key(seed), 9)
    return {
        "prior_state": gaussian(streams_of[0], (ENSEMBLE_SIZE, FIELD_NUMBER, MERIDIAN_POINTS, ZONAL_POINTS), 1.0, 6.0, ((0, 8), (2, 4))),
        "norm_scale": jnp.clip(1.0 + 0.18 * jax.random.normal(streams_of[1], (FIELD_NUMBER,), jnp.float32), 0.1, 1.9),
        "entry_kernel": gaussian(streams_of[2], (9, F, FIELD_NUMBER), (9 * FIELD_NUMBER) ** -0.5, 0.25),
        "closing_filter": gaussian(streams_of[3], (9, FIELD_NUMBER, F), (9 * F) ** -0.5, 0.125),
        "observed_cell": set_ends(jax.random.randint(streams_of[4], (ZONAL_SECTORS, PARALLEL_STRIPS, OBS_DEV), 0, CELLS_REG), jax.random.fold_in(streams_of[4], 1), 0, CELLS_REG - 1).astype(jnp.int32),
        "observed_weight": gaussian(streams_of[5], (ZONAL_SECTORS, PARALLEL_STRIPS, OBS_DEV, FIELD_NUMBER), FIELD_NUMBER ** -0.5, 0.75, ((0, 8), (1, 4)), jnp.float32),
        "observed_value": gaussian(streams_of[6], (ZONAL_SECTORS, PARALLEL_STRIPS, OBS_DEV), 1.0, 6.0, ((0, 8), (1, 4)), jnp.float32),
        "observed_precision": jnp.clip(jnp.exp(math.log(2.0) - 2.0794415 * jax.random.uniform(streams_of[7], (ZONAL_SECTORS, PARALLEL_STRIPS, OBS_DEV), jnp.float32) ** shard_levels(streams_of[7], (ZONAL_SECTORS, PARALLEL_STRIPS, OBS_DEV), ((0, 8), (1, 4)), -0.2, 0.2)), 0.25, 2.0),
    }


highest = lax.Precision.HIGHEST

def entry_convolve(padded, weights, tally_lines):
    windows = []
    for offset in range(9):
        row_off = offset // 3
        col_off = offset % 3
        window = padded[:, :, row_off:row_off + tally_lines, :]
        if col_off != 1:
            window = jnp.roll(window, 1 - col_off, axis=3)
        windows.append(window)
    stacked = jnp.concatenate(windows, axis=1)
    outputs = weights.shape[1]
    flat_kernel = jnp.transpose(weights, (1, 0, 2)).reshape(outputs, -1)
    return jnp.einsum('ok,mkyx->moyx', flat_kernel, stacked, preferred_element_type=jnp.float32)

def closing_convolve(padded, weights, tally_lines):
    running = None
    for row_off in range(3):
        window = padded[:, :, row_off:row_off + tally_lines, :]
        products = jnp.einsum('boc,mcyx->mboyx', weights[3 * row_off:3 * row_off + 3], window, preferred_element_type=jnp.float32)
        for col_off in range(3):
            part = products[:, col_off]
            if col_off != 1:
                part = jnp.roll(part, 1 - col_off, axis=3)
            running = part if running is None else running + part
    return running

def inverse_root(gram, members):
    identity = jnp.eye(members, dtype=jnp.float32)
    matrix = identity + gram / (members - 1)
    magnitude = jnp.sqrt(jnp.sum(matrix * matrix))
    current = matrix / magnitude
    inverse = identity
    for sweep_index in range(NS_ITERS):
        factor = 0.5 * (3.0 * identity - jnp.dot(inverse, current, precision=highest))
        if sweep_index + 1 < NS_ITERS:
            current = jnp.dot(current, factor, precision=highest)
        inverse = jnp.dot(factor, inverse, precision=highest)
    return inverse / jnp.sqrt(magnitude)

def reference(prior_state, norm_scale, entry_kernel, closing_filter, observed_cell, observed_weight, observed_value, observed_precision):
    member_layer = 8
    stencil_sequence = prior_state.reshape(ENSEMBLE_SIZE // member_layer, member_layer, FIELD_NUMBER, MERIDIAN_POINTS, ZONAL_POINTS)
    row_pad = ((0, 0), (0, 0), (1, 1), (0, 0))

    def predictive_stencil(stacked_fields):
        solitary_fields = stacked_fields.astype(jnp.float32)
        inverse = lax.rsqrt(lax.optimization_barrier(jnp.mean(solitary_fields * solitary_fields, axis=1, keepdims=True)) + 1e-06)
        normed = (solitary_fields * inverse * norm_scale[None, :, None, None]).astype(jnp.bfloat16)
        padded = jnp.pad(normed, row_pad)
        hidden = jax.nn.gelu(entry_convolve(padded, entry_kernel, MERIDIAN_POINTS)).astype(jnp.bfloat16)
        ghost_border = jnp.pad(hidden, row_pad)
        return (solitary_fields + closing_convolve(ghost_border, closing_filter, MERIDIAN_POINTS)).astype(jnp.bfloat16)
    advance_prediction = lax.map(predictive_stencil, stencil_sequence).reshape(ENSEMBLE_SIZE, FIELD_NUMBER, MERIDIAN_POINTS, ZONAL_POINTS)
    partition_strips = advance_prediction.reshape(ENSEMBLE_SIZE, FIELD_NUMBER, PARALLEL_STRIPS, STRIP_HEIGHT, ZONAL_SECTORS, SECTOR_WIDTH).transpose(2, 4, 5, 3, 1, 0)
    inputs = (partition_strips, observed_cell.transpose(1, 0, 2), observed_weight.transpose(1, 0, 2, 3), observed_value.transpose(1, 0, 2), observed_precision.transpose(1, 0, 2))

    def analyse(pieces):
        band_state, located, obs_w, values, obs_prec = pieces
        states = band_state.astype(jnp.float32).reshape(ZONAL_SECTORS, REGION_ROWS, ENSEMBLE_SIZE)
        center = lax.optimization_barrier(jnp.mean(states, axis=2, keepdims=True))
        perturb = states - center
        onehot = (located[:, :, None] == lax.iota(jnp.int32, CELLS_REG)[None, None, :]).astype(jnp.float32)
        operator = (onehot[:, :, :, None] * obs_w[:, :, None, :]).reshape(ZONAL_SECTORS, OBS_DEV, REGION_ROWS)
        obs_pert = jnp.einsum('gok,gkm->gom', operator, perturb, precision=highest)
        innovation = values - jnp.einsum('gok,gk->go', operator, center[:, :, 0], precision=highest)
        weighted = obs_pert * obs_prec[:, :, None]
        gram = jnp.einsum('gom,gon->mn', weighted, obs_pert, precision=highest)
        proj = jnp.einsum('go,gom->m', innovation * obs_prec, obs_pert, precision=highest)
        transform = inverse_root(gram, ENSEMBLE_SIZE)
        mean_shift = jnp.dot(transform, jnp.dot(transform, proj, precision=highest), precision=highest) / (ENSEMBLE_SIZE - 1)
        analysed = center + jnp.einsum('grm,mn->grn', perturb, transform + mean_shift[:, None], precision=highest)
        return analysed.reshape(ZONAL_SECTORS, SECTOR_WIDTH, STRIP_HEIGHT, FIELD_NUMBER, ENSEMBLE_SIZE)
    result = lax.map(analyse, inputs)
    return result.transpose(1, 2, 0, 3, 4, 5).reshape(ZONAL_POINTS, MERIDIAN_POINTS, FIELD_NUMBER, ENSEMBLE_SIZE)
```

```python
import functools
import math

import jax
import jax.numpy as jnp
from jax import lax
from jax.experimental import pallas as pl
from jax.experimental.pallas import tpu as pltpu
from jax.sharding import PartitionSpec as P

NS_ITERS = 3
LANES = 128
MESH = pl.DeviceIdType.MESH
VMEM_LIMIT = 56 * 1024 * 1024
F32 = jnp.float32
BF16 = jnp.bfloat16
highest = lax.Precision.HIGHEST


def halo_kernel(own_ref, below_ref, above_ref, send_sem, recv_sem):
    bands = lax.axis_size("lat")
    band = lax.axis_index("lat")
    barrier = pltpu.get_barrier_semaphore()

    @pl.when(band > 0)
    def _():
        pl.semaphore_signal(barrier, inc=1, device_id={"lat": band - 1}, device_id_type=MESH)

    @pl.when(band < bands - 1)
    def _():
        pl.semaphore_signal(barrier, inc=1, device_id={"lat": band + 1}, device_id_type=MESH)

    peers = jnp.where(band > 0, 1, 0) + jnp.where(band < bands - 1, 1, 0)
    pl.semaphore_wait(barrier, peers)

    down = pltpu.make_async_remote_copy(
        own_ref, above_ref, send_sem.at[0], recv_sem.at[0],
        device_id={"lat": band - 1}, device_id_type=MESH,
    )
    up = pltpu.make_async_remote_copy(
        own_ref, below_ref, send_sem.at[1], recv_sem.at[1],
        device_id={"lat": band + 1}, device_id_type=MESH,
    )

    @pl.when(band > 0)
    def _():
        down.start()

    @pl.when(band < bands - 1)
    def _():
        up.start()

    @pl.when(band > 0)
    def _():
        down.wait_send()
        up.wait_recv()

    @pl.when(band < bands - 1)
    def _():
        up.wait_send()
        down.wait_recv()


def halo_exchange(own):
    shape = jax.ShapeDtypeStruct(own.shape, own.dtype)
    anywhere = pl.BlockSpec(memory_space=pl.ANY)
    return pl.pallas_call(
        halo_kernel,
        out_shape=(shape, shape),
        in_specs=[anywhere],
        out_specs=(anywhere, anywhere),
        scratch_shapes=[pltpu.SemaphoreType.DMA((2,)), pltpu.SemaphoreType.DMA((2,))],
        compiler_params=pltpu.CompilerParams(collective_id=0, has_side_effects=True),
        name="halo",
    )(own)


def greet_all(axis):
    count = lax.axis_size(axis)
    me = lax.axis_index(axis)
    barrier = pltpu.get_barrier_semaphore()
    for step in range(1, count):
        pl.semaphore_signal(
            barrier, inc=1, device_id={axis: lax.rem(me + step, count)}, device_id_type=MESH
        )
    pl.semaphore_wait(barrier, count - 1)


def exchange_kernel(parts_ref, got_ref, send_sem, recv_sem, own_sem):
    count = lax.axis_size("mem")
    me = lax.axis_index("mem")
    greet_all("mem")
    copies = []
    for step in range(1, count):
        other = lax.rem(me + step, count)
        copy = pltpu.make_async_remote_copy(
            parts_ref.at[other], got_ref.at[me], send_sem.at[step], recv_sem.at[step],
            device_id={"mem": other}, device_id_type=MESH,
        )
        copy.start()
        copies.append(copy)
    keep = pltpu.make_async_copy(parts_ref.at[me], got_ref.at[me], own_sem)
    keep.start()
    keep.wait()
    for copy in copies:
        copy.wait()


def exchange(parts):
    count = parts.shape[0]
    anywhere = pl.BlockSpec(memory_space=pl.ANY)
    return pl.pallas_call(
        exchange_kernel,
        out_shape=jax.ShapeDtypeStruct(parts.shape, parts.dtype),
        in_specs=[anywhere],
        out_specs=anywhere,
        scratch_shapes=[
            pltpu.SemaphoreType.DMA((count,)),
            pltpu.SemaphoreType.DMA((count,)),
            pltpu.SemaphoreType.DMA,
        ],
        compiler_params=pltpu.CompilerParams(collective_id=1, has_side_effects=True),
        name="exchange",
    )(parts)


def gather_kernel(mine_ref, all_ref, send_sem, recv_sem, own_sem):
    count = lax.axis_size("mem")
    me = lax.axis_index("mem")
    greet_all("mem")
    copies = []
    for step in range(1, count):
        other = lax.rem(me + step, count)
        copy = pltpu.make_async_remote_copy(
            mine_ref, all_ref.at[me], send_sem.at[step], recv_sem.at[step],
            device_id={"mem": other}, device_id_type=MESH,
        )
        copy.start()
        copies.append(copy)
    keep = pltpu.make_async_copy(mine_ref, all_ref.at[me], own_sem)
    keep.start()
    keep.wait()
    for copy in copies:
        copy.wait()


def gather(mine, count):
    return pl.pallas_call(
        gather_kernel,
        out_shape=jax.ShapeDtypeStruct((count,) + mine.shape, mine.dtype),
        in_specs=[pl.BlockSpec(memory_space=pltpu.VMEM)],
        out_specs=pl.BlockSpec(memory_space=pltpu.VMEM),
        scratch_shapes=[
            pltpu.SemaphoreType.DMA((count,)),
            pltpu.SemaphoreType.DMA((count,)),
            pltpu.SemaphoreType.DMA,
        ],
        compiler_params=pltpu.CompilerParams(collective_id=2, has_side_effects=True),
        name="gather",
    )(mine)


def forecast_kernel(
    groups, own_ref, below_ref, above_ref, gain_ref, entry_ref, closing_ref,
    parts_ref, stack, field,
):
    members, rows, width = own_ref.shape
    band = lax.axis_index("lat")
    bands = lax.axis_size("lat")
    has_below = band > 0
    has_above = band < bands - 1
    gain = gain_ref[...]
    half_below = jnp.where(has_below, 0.5, 0.0).astype(F32)
    half_above = jnp.where(has_above, 0.5, 0.0).astype(F32)

    def normed(ref, member):
        values = ref[member].astype(F32).reshape(rows // 8, 8, width)
        square = jnp.sum(values * values, axis=0)
        square = square + pltpu.roll(square, 2, 0)
        square = square + pltpu.roll(square, 4, 0)
        inverse = lax.rsqrt(square * (2.0 / rows) + 1e-06)
        return (values * inverse[None]).reshape(rows, width) * gain

    def gelu(value, half):
        inner = math.sqrt(2.0 / math.pi) * (value + 0.044715 * (value * value * value))
        return ((half * value) * (1.0 + jnp.tanh(inner))).astype(BF16)

    pair = 2
    half_rows = entry_ref.shape[0] // 2
    depth = entry_ref.shape[1] // 2
    for first in range(0, members, pair):
        for which in range(pair):
            lanes = slice(which * width, (which + 1) * width)
            for block, (ref, valid) in enumerate(
                ((below_ref, has_below), (own_ref, None), (above_ref, has_above))
            ):
                value = normed(ref, first + which)
                if valid is not None:
                    value = jnp.where(valid, value, 0.0)
                for tap in range(3):
                    moved = value if tap == 1 else pltpu.roll(value, (1 - tap) % width, 1)
                    start = block * depth + tap * rows
                    stack[start : start + rows, lanes] = moved.astype(BF16)
        entry = entry_ref[...]
        low = jnp.dot(entry, stack[: 2 * depth, :], preferred_element_type=F32)
        high = jnp.dot(entry, stack[depth:, :], preferred_element_type=F32)
        hidden = jnp.concatenate(
            [
                gelu(low[:half_rows], half_below),
                gelu(low[half_rows:], 0.5),
                gelu(high[:half_rows], 0.5),
                gelu(high[half_rows:], half_above),
            ],
            axis=0,
        )
        products = jnp.dot(closing_ref[...], hidden, preferred_element_type=F32)
        for which in range(pair):
            lanes = slice(which * width, (which + 1) * width)
            total = own_ref[first + which].astype(F32)
            for tap in range(3):
                part = products[tap * rows : (tap + 1) * rows, lanes]
                total = total + (part if tap == 1 else pltpu.roll(part, (1 - tap) % width, 1))
            field[(first + which) * rows : (first + which + 1) * rows, :] = total

    columns = width // groups
    lane_group = lax.broadcasted_iota(jnp.int32, (members, width), 1) // columns
    pieces = rows // (2 * groups)
    for piece in range(pieces):
        for line in range(2):
            tiles = [
                field[pl.ds(piece * groups * 2 + inner * 2 + line, members, stride=rows), :]
                for inner in range(groups)
            ]
            step = 1
            while step < groups:
                keep_low = (lane_group // step) % 2 == 0
                turned = list(tiles)
                for index in range(groups):
                    if (index // step) % 2 == 0:
                        a, b = tiles[index], tiles[index + step]
                        turned[index] = jnp.where(keep_low, a, pltpu.roll(b, step * columns, 1))
                        turned[index + step] = jnp.where(
                            keep_low, pltpu.roll(a, width - step * columns, 1), b
                        )
                tiles = turned
                step *= 2
            for group in range(groups):
                parts_ref[group, piece * 2 + line] = tiles[group].astype(BF16)


def forecast(own, below, above, gain, entry, closing, groups):
    members, rows, width = own.shape
    chunk = min(16, members)
    pieces = rows // groups
    block = pl.BlockSpec((chunk, rows, width), lambda i: (i, 0, 0))
    whole = lambda a: pl.BlockSpec(a.shape, lambda i: (0,) * a.ndim)
    return pl.pallas_call(
        functools.partial(forecast_kernel, groups),
        out_shape=jax.ShapeDtypeStruct((groups, pieces, members, width), BF16),
        grid=(members // chunk,),
        in_specs=[block, block, block, whole(gain), whole(entry), whole(closing)],
        out_specs=pl.BlockSpec((groups, pieces, chunk, width), lambda i: (0, 0, i, 0)),
        scratch_shapes=[
            pltpu.VMEM((9 * rows, 2 * width), BF16),
            pltpu.VMEM((chunk * rows, width), F32),
        ],
        compiler_params=pltpu.CompilerParams(vmem_limit_bytes=VMEM_LIMIT),
        name="forecast",
    )(own, below, above, gain, entry, closing)


def observe_kernel(got_ref, operator_ref, value_ref, precision_ref, out_ref):
    sources, pieces, part, width = got_ref.shape
    observations = operator_ref.shape[1]
    total = None
    for piece in range(pieces):
        operator = operator_ref[piece]
        high = operator.astype(BF16)
        rest = operator - high.astype(F32)
        middle = rest.astype(BF16)
        low = (rest - middle.astype(F32)).astype(BF16)
        stacked = jnp.concatenate([high, middle, low], axis=0)
        states = got_ref[:, piece].reshape(sources * part, width)
        term = lax.dot_general(
            stacked, states, (((1,), (1,)), ((), ())), preferred_element_type=F32
        )
        total = term if total is None else total + term
    seen = total[:observations] + (total[observations : 2 * observations] + total[2 * observations :])
    mean = jnp.mean(seen, axis=1, keepdims=True)
    root = jnp.sqrt(precision_ref[...])
    out_ref[:, : sources * part] = (seen - mean) * root[:, :1]
    out_ref[:, sources * part :] = (value_ref[...] - mean) * root


def observe(got, operator, value, precision):
    sources, _, part, width = got.shape
    observations = operator.shape[1]
    return pl.pallas_call(
        observe_kernel,
        out_shape=jax.ShapeDtypeStruct((observations, sources * part + LANES), F32),
        compiler_params=pltpu.CompilerParams(vmem_limit_bytes=VMEM_LIMIT),
        name="observe",
    )(got, operator, value, precision)


def weights_of(gathered, members):
    u = gathered[:, :members] * (1.0 / math.sqrt(members - 1))
    innovation = gathered[:, members:]
    count = u.shape[0]
    dot = functools.partial(jnp.dot, precision=highest, preferred_element_type=F32)
    g = lax.dot_general(u, u, (((1,), (1,)), ((), ())), precision=highest, preferred_element_type=F32)
    eye = (
        lax.broadcasted_iota(jnp.int32, (count, count), 0)
        == lax.broadcasted_iota(jnp.int32, (count, count), 1)
    ).astype(F32)
    total = lambda a: jnp.sum(jnp.sum(a, axis=1, keepdims=True), axis=0, keepdims=True)
    square = total(g * (g + 2.0 * eye)) + float(members)
    magnitude = jnp.sqrt(square)
    y_c, y_m = 1.0 / magnitude, eye / magnitude
    z_c, z_m = jnp.ones_like(magnitude), None
    for sweep in range(NS_ITERS):
        if z_m is None:
            p_m = y_m
        else:
            gy = dot(g, y_m)
            p_m = z_c * y_m + y_c * z_m + dot(z_m, gy)
        t_c, t_m = 0.5 * (3.0 - z_c * y_c), -0.5 * p_m
        gt = dot(g, t_m)
        if sweep + 1 < NS_ITERS:
            y_c, y_m = y_c * t_c, y_c * t_m + t_c * y_m + dot(y_m, gt)
        if z_m is None:
            z_c, z_m = t_c * z_c, z_c * t_m
        else:
            z_c, z_m = t_c * z_c, t_c * z_m + z_c * t_m + dot(z_m, gt)
    scale = lax.rsqrt(magnitude)
    a_c, a_m = z_c * scale, z_m * scale
    once = a_c * innovation + dot(a_m, dot(g, innovation))
    twice = a_c * once + dot(a_m, dot(g, once))
    v = dot(a_m, u) + twice[:, :1] * (1.0 / math.sqrt(members - 1))
    full = lax.dot_general(u, v, (((0,), (0,)), ((), ())), precision=highest, preferred_element_type=F32)
    diagonal = lax.broadcasted_iota(jnp.int32, (members, members), 0) == lax.broadcasted_iota(
        jnp.int32, (members, members), 1
    )
    full = full + jnp.where(diagonal, a_c, 0.0)
    column = jnp.sum(full, axis=0, keepdims=True)
    return full + (1.0 - column) * (1.0 / members)


def analyse_kernel(got_ref, gathered_ref, out_ref, coarse, fine, turned):
    sources, _, part, width = got_ref.shape
    members = sources * part
    columns, lines, inner, _ = out_ref.shape

    @pl.when(pl.program_id(0) == 0)
    def _():
        full = weights_of(gathered_ref[...], members)
        high = full.astype(BF16)
        coarse[...] = high
        fine[...] = (full - high.astype(F32)).astype(BF16)

    turn = (((0,), (0,)), ((), ()))
    for line in range(lines):
        states = got_ref[:, line].reshape(members, width)
        result = lax.dot_general(states, coarse[...], turn, preferred_element_type=F32)
        result += lax.dot_general(states, fine[...], turn, preferred_element_type=F32)
        for index in range(inner):
            rows = result[index * columns : (index + 1) * columns]
            for tile in range(members // LANES):
                turned[tile, pl.ds(line * inner + index, columns, stride=lines * inner), :] = rows[
                    :, tile * LANES : (tile + 1) * LANES
                ]
    for tile in range(members // LANES):
        out_ref[:, :, :, tile * LANES : (tile + 1) * LANES] = turned[tile].reshape(
            columns, lines, inner, LANES
        )


def analyse(got, gathered, columns, variables):
    sources, _, part, width = got.shape
    members = sources * part
    inner = width // columns
    return pl.pallas_call(
        analyse_kernel,
        out_shape=jax.ShapeDtypeStruct((columns, 2, variables, members), F32),
        grid=(variables // inner,),
        in_specs=[
            pl.BlockSpec((sources, 2, part, width), lambda i: (0, i, 0, 0)),
            pl.BlockSpec(gathered.shape, lambda i: (0, 0)),
        ],
        out_specs=pl.BlockSpec((columns, 2, inner, members), lambda i: (0, 0, i, 0)),
        scratch_shapes=[
            pltpu.VMEM((members, members), BF16),
            pltpu.VMEM((members, members), BF16),
            pltpu.VMEM((members // LANES, columns * 2 * inner, LANES), F32),
        ],
        compiler_params=pltpu.CompilerParams(vmem_limit_bytes=VMEM_LIMIT),
        name="analyse",
    )(got, gathered)


def on_device(
    prior_state,
    norm_scale,
    entry_kernel,
    closing_filter,
    observed_cell,
    observed_weight,
    observed_value,
    observed_precision,
):
    groups = lax.axis_size("mem")
    members, variables, lines, width = prior_state.shape
    hidden = entry_kernel.shape[1]
    columns = width // groups
    own = prior_state.reshape(members, variables * lines, width)
    gain = jnp.broadcast_to(jnp.repeat(norm_scale, lines)[:, None], (variables * lines, width))

    taps = entry_kernel.reshape(3, 3, hidden, variables)
    by_line = jnp.stack([jnp.pad(taps, ((j, 1 - j), (0, 0), (0, 0), (0, 0))) for j in range(2)])
    entry = by_line.reshape(2, 2, 2, 3, hidden, variables)
    entry = jnp.transpose(entry, (0, 4, 1, 3, 5, 2)).reshape(2 * hidden, 12 * variables)
    taps = closing_filter.reshape(3, 3, variables, hidden)
    by_line = jnp.stack([jnp.pad(taps, ((y, 1 - y), (0, 0), (0, 0), (0, 0))) for y in range(2)])
    closing = jnp.transpose(by_line, (2, 3, 0, 1, 4)).reshape(6 * variables, 4 * hidden)

    located = observed_cell[0, 0]
    observations = located.shape[0]
    cells = (located[:, None] == lax.iota(jnp.int32, columns * lines)[None, :]).astype(F32)
    cells = jnp.transpose(cells.reshape(observations, columns, lines), (2, 0, 1))
    weight = observed_weight[0, 0].reshape(observations, variables // groups, groups)
    operator = (
        jnp.transpose(weight, (1, 0, 2))[:, None, :, :, None] * cells[None, :, :, None, :]
    ).reshape(variables // groups * lines, observations, groups * columns)
    value = jnp.broadcast_to(observed_value[0, 0][:, None], (observations, LANES))
    precision = jnp.broadcast_to(observed_precision[0, 0][:, None], (observations, LANES))

    below, above = halo_exchange(own)
    parts = forecast(own, below, above, gain, entry, closing, groups)
    got = exchange(parts)
    mine = observe(got, operator, value, precision)
    gathered = gather(mine, groups)
    gathered = gathered.reshape(groups * observations, mine.shape[1])
    return analyse(got, gathered, columns, variables)


def solution(mesh):
    return jax.shard_map(
        on_device,
        mesh=mesh,
        in_specs=(
            P("mem", None, "lat", None),
            P(),
            P(),
            P(),
            P("mem", "lat", None),
            P("mem", "lat", None, None),
            P("mem", "lat", None),
            P("mem", "lat", None),
        ),
        out_specs=P("mem", "lat", None, None),
        check_vma=False,
    )
```

```python
import functools
import math

import jax
import jax.numpy as jnp
from jax import lax
from jax.experimental import pallas as pl
from jax.experimental.pallas import tpu as pltpu
from jax.sharding import PartitionSpec as P

NS_ITERS = 3
LANES = 128
MESH = pl.DeviceIdType.MESH
VMEM_LIMIT = 56 * 1024 * 1024
F32 = jnp.float32
BF16 = jnp.bfloat16
highest = lax.Precision.HIGHEST


def greet_all(axis):
    count = lax.axis_size(axis)
    me = lax.axis_index(axis)
    barrier = pltpu.get_barrier_semaphore()
    for step in range(1, count):
        pl.semaphore_signal(
            barrier, inc=1, device_id={axis: lax.rem(me + step, count)}, device_id_type=MESH
        )
    pl.semaphore_wait(barrier, count - 1)


def gather_kernel(mine_ref, all_ref, send_sem, recv_sem, own_sem):
    count = lax.axis_size("mem")
    me = lax.axis_index("mem")
    greet_all("mem")
    copies = []
    for step in range(1, count):
        other = lax.rem(me + step, count)
        copy = pltpu.make_async_remote_copy(
            mine_ref, all_ref.at[me], send_sem.at[step], recv_sem.at[step],
            device_id={"mem": other}, device_id_type=MESH,
        )
        copy.start()
        copies.append(copy)
    keep = pltpu.make_async_copy(mine_ref, all_ref.at[me], own_sem)
    keep.start()
    keep.wait()
    for copy in copies:
        copy.wait()


def gather(mine, count):
    return pl.pallas_call(
        gather_kernel,
        out_shape=jax.ShapeDtypeStruct((count,) + mine.shape, mine.dtype),
        in_specs=[pl.BlockSpec(memory_space=pltpu.VMEM)],
        out_specs=pl.BlockSpec(memory_space=pltpu.VMEM),
        scratch_shapes=[
            pltpu.SemaphoreType.DMA((count,)),
            pltpu.SemaphoreType.DMA((count,)),
            pltpu.SemaphoreType.DMA,
        ],
        compiler_params=pltpu.CompilerParams(collective_id=2, has_side_effects=True),
        name="gather",
    )(mine)


def forecast_kernel(
    own_ref, gain_ref, entry_ref, closing_ref, prior_ref, got_ref,
    below_ref, above_ref, parts_ref, stack, field,
    halo_send, halo_recv, part_send, part_recv, keep_sem,
):
    members, rows, width = own_ref.shape
    chunks = pl.num_programs(0)
    chunk_count = parts_ref.shape[0]
    chunk = pl.program_id(0)
    groups = lax.axis_size("mem")
    me = lax.axis_index("mem")
    band = lax.axis_index("lat")
    bands = lax.axis_size("lat")
    has_below = band > 0
    has_above = band < bands - 1

    def to_lower(index):
        piece = pl.ds(index * members, members)
        return pltpu.make_async_remote_copy(
            prior_ref.at[piece], above_ref.at[piece], halo_send.at[0, index], halo_recv.at[0, index],
            device_id={"lat": band - 1}, device_id_type=MESH,
        )

    def to_upper(index):
        piece = pl.ds(index * members, members)
        return pltpu.make_async_remote_copy(
            prior_ref.at[piece], below_ref.at[piece], halo_send.at[1, index], halo_recv.at[1, index],
            device_id={"lat": band + 1}, device_id_type=MESH,
        )

    def to_group(index, step):
        other = lax.rem(me + step, groups)
        return pltpu.make_async_remote_copy(
            parts_ref.at[index, other], got_ref.at[me, :, pl.ds(index * members, members)],
            part_send.at[index, step], part_recv.at[index, step],
            device_id={"mem": other}, device_id_type=MESH,
        )

    def to_self(index):
        return pltpu.make_async_copy(
            parts_ref.at[index, me], got_ref.at[me, :, pl.ds(index * members, members)],
            keep_sem.at[index],
        )

    @pl.when(chunk == 0)
    def _():
        barrier = pltpu.get_barrier_semaphore()
        for step in range(1, groups):
            pl.semaphore_signal(
                barrier, inc=1, device_id={"mem": lax.rem(me + step, groups)}, device_id_type=MESH
            )

        @pl.when(has_below)
        def _():
            pl.semaphore_signal(barrier, inc=1, device_id={"lat": band - 1}, device_id_type=MESH)

        @pl.when(has_above)
        def _():
            pl.semaphore_signal(barrier, inc=1, device_id={"lat": band + 1}, device_id_type=MESH)

        peers = jnp.where(has_below, 1, 0) + jnp.where(has_above, 1, 0)
        pl.semaphore_wait(barrier, groups - 1 + peers)
        for index in range(chunk_count):

            @pl.when(has_below)
            def _():
                to_lower(index).start()

            @pl.when(has_above)
            def _():
                to_upper(index).start()

    @pl.when(has_below)
    def _():
        to_upper(chunk).wait_recv()

    @pl.when(has_above)
    def _():
        to_lower(chunk).wait_recv()

    gain = gain_ref[...]
    half_below = jnp.where(has_below, 0.5, 0.0).astype(F32)
    half_above = jnp.where(has_above, 0.5, 0.0).astype(F32)

    def normed(values):
        values = values.astype(F32).reshape(rows // 8, 8, width)
        square = jnp.sum(values * values, axis=0)
        square = square + pltpu.roll(square, 2, 0)
        square = square + pltpu.roll(square, 4, 0)
        inverse = lax.rsqrt(square * (2.0 / rows) + 1e-06)
        return (values * inverse[None]).reshape(rows, width) * gain

    def gelu(value, half):
        inner = math.sqrt(2.0 / math.pi) * (value + 0.044715 * (value * value * value))
        return ((half * value) * (1.0 + jnp.tanh(inner))).astype(BF16)

    pair = 2
    slots = stack.shape[0]
    half_rows = entry_ref.shape[0] // 2
    depth = entry_ref.shape[1] // 2

    def convolve(first, slot):
        for which in range(pair):
            lanes = slice(which * width, (which + 1) * width)
            member = first + which
            for block, (read, valid) in enumerate(
                (
                    (lambda: below_ref[chunk * members + member], has_below),
                    (lambda: own_ref[member], None),
                    (lambda: above_ref[chunk * members + member], has_above),
                )
            ):
                value = normed(read())
                if valid is not None:
                    value = jnp.where(valid, value, 0.0)
                for tap in range(3):
                    moved = value if tap == 1 else pltpu.roll(value, (1 - tap) % width, 1)
                    start = block * depth + tap * rows
                    stack[slot, start : start + rows, lanes] = moved.astype(BF16)
        entry = entry_ref[...]
        low = jnp.dot(entry, stack[slot, : 2 * depth, :], preferred_element_type=F32)
        high = jnp.dot(entry, stack[slot, depth:, :], preferred_element_type=F32)
        hidden = jnp.concatenate(
            [
                gelu(low[:half_rows], half_below),
                gelu(low[half_rows:], 0.5),
                gelu(high[:half_rows], 0.5),
                gelu(high[half_rows:], half_above),
            ],
            axis=0,
        )
        products = jnp.dot(closing_ref[...], hidden, preferred_element_type=F32)
        for which in range(pair):
            lanes = slice(which * width, (which + 1) * width)
            total = own_ref[first + which].astype(F32)
            for tap in range(3):
                part = products[tap * rows : (tap + 1) * rows, lanes]
                total = total + (part if tap == 1 else pltpu.roll(part, (1 - tap) % width, 1))
            field[pl.ds(pl.multiple_of((first + which) * rows, rows), rows), :] = total

    @pl.loop(0, members // (pair * slots))
    def _(turn):
        for slot in range(slots):
            convolve((turn * slots + slot) * pair, slot)

    columns = width // groups
    lane_group = lax.broadcasted_iota(jnp.int32, (members, width), 1) // columns

    @pl.loop(0, rows // (2 * groups))
    def _(piece):
        for line in range(2):
            tiles = [
                field[pl.ds(piece * (groups * 2) + (inner * 2 + line), members, stride=rows), :]
                for inner in range(groups)
            ]
            step = 1
            while step < groups:
                keep_low = (lane_group // step) % 2 == 0
                turned = list(tiles)
                for index in range(groups):
                    if (index // step) % 2 == 0:
                        a, b = tiles[index], tiles[index + step]
                        turned[index] = jnp.where(keep_low, a, pltpu.roll(b, step * columns, 1))
                        turned[index + step] = jnp.where(
                            keep_low, pltpu.roll(a, width - step * columns, 1), b
                        )
                tiles = turned
                step *= 2
            for group in range(groups):
                parts_ref[chunk, group, piece * 2 + line] = tiles[group].astype(BF16)

    for step in range(1, groups):
        to_group(chunk, step).start()
    to_self(chunk).start()

    @pl.when(chunk == chunks - 1)
    def _():
        for index in range(chunk_count):

            @pl.when(has_below)
            def _():
                to_lower(index).wait_send()

            @pl.when(has_above)
            def _():
                to_upper(index).wait_send()

            for step in range(1, groups):
                to_group(index, step).wait()
            to_self(index).wait()


def forecast(own, gain, entry, closing, groups):
    members, rows, width = own.shape
    chunk = min(16, members)
    chunks = members // chunk
    pieces = rows // groups
    whole = lambda a: pl.BlockSpec(a.shape, lambda i: (0,) * a.ndim)
    anywhere = pl.BlockSpec(memory_space=pl.ANY)
    return pl.pallas_call(
        forecast_kernel,
        out_shape=jax.ShapeDtypeStruct((groups, pieces, members, width), BF16),
        grid=(chunks,),
        in_specs=[
            pl.BlockSpec((chunk, rows, width), lambda i: (i, 0, 0)),
            whole(gain), whole(entry), whole(closing), anywhere,
        ],
        out_specs=anywhere,
        scratch_shapes=[
            pltpu.VMEM((members, rows, width), BF16),
            pltpu.VMEM((members, rows, width), BF16),
            pltpu.VMEM((chunks, groups, pieces, chunk, width), BF16),
            pltpu.VMEM((2, 9 * rows, 2 * width), BF16),
            pltpu.VMEM((chunk * rows, width), F32),
            pltpu.SemaphoreType.DMA((2, chunks)),
            pltpu.SemaphoreType.DMA((2, chunks)),
            pltpu.SemaphoreType.DMA((chunks, groups)),
            pltpu.SemaphoreType.DMA((chunks, groups)),
            pltpu.SemaphoreType.DMA((chunks,)),
        ],
        compiler_params=pltpu.CompilerParams(
            vmem_limit_bytes=VMEM_LIMIT, collective_id=0, has_side_effects=True
        ),
        name="forecast",
    )(own, gain, entry, closing, own)


def observe_kernel(got_ref, operator_ref, value_ref, precision_ref, out_ref):
    sources, pieces, part, width = got_ref.shape
    observations = operator_ref.shape[1]
    total = None
    for piece in range(pieces):
        operator = operator_ref[piece]
        high = operator.astype(BF16)
        rest = operator - high.astype(F32)
        middle = rest.astype(BF16)
        low = (rest - middle.astype(F32)).astype(BF16)
        stacked = jnp.concatenate([high, middle, low], axis=0)
        states = got_ref[:, piece].reshape(sources * part, width)
        term = lax.dot_general(
            stacked, states, (((1,), (1,)), ((), ())), preferred_element_type=F32
        )
        total = term if total is None else total + term
    seen = total[:observations] + (total[observations : 2 * observations] + total[2 * observations :])
    mean = jnp.mean(seen, axis=1, keepdims=True)
    root = jnp.sqrt(precision_ref[...])
    out_ref[:, : sources * part] = (seen - mean) * root[:, :1]
    out_ref[:, sources * part :] = (value_ref[...] - mean) * root


def observe(got, operator, value, precision):
    sources, _, part, width = got.shape
    observations = operator.shape[1]
    return pl.pallas_call(
        observe_kernel,
        out_shape=jax.ShapeDtypeStruct((observations, sources * part + LANES), F32),
        compiler_params=pltpu.CompilerParams(vmem_limit_bytes=VMEM_LIMIT),
        name="observe",
    )(got, operator, value, precision)


def weights_of(gathered, members):
    u = gathered[:, :members] * (1.0 / math.sqrt(members - 1))
    innovation = gathered[:, members:]
    count = u.shape[0]
    dot = functools.partial(jnp.dot, precision=highest, preferred_element_type=F32)
    g = lax.dot_general(u, u, (((1,), (1,)), ((), ())), precision=highest, preferred_element_type=F32)
    eye = (
        lax.broadcasted_iota(jnp.int32, (count, count), 0)
        == lax.broadcasted_iota(jnp.int32, (count, count), 1)
    ).astype(F32)
    total = lambda a: jnp.sum(jnp.sum(a, axis=1, keepdims=True), axis=0, keepdims=True)
    square = total(g * (g + 2.0 * eye)) + float(members)
    magnitude = jnp.sqrt(square)
    y_c, y_m = 1.0 / magnitude, eye / magnitude
    z_c, z_m = jnp.ones_like(magnitude), None
    for sweep in range(NS_ITERS):
        if z_m is None:
            p_m = y_m
        else:
            gy = dot(g, y_m)
            p_m = z_c * y_m + y_c * z_m + dot(z_m, gy)
        t_c, t_m = 0.5 * (3.0 - z_c * y_c), -0.5 * p_m
        gt = dot(g, t_m)
        if sweep + 1 < NS_ITERS:
            y_c, y_m = y_c * t_c, y_c * t_m + t_c * y_m + dot(y_m, gt)
        if z_m is None:
            z_c, z_m = t_c * z_c, z_c * t_m
        else:
            z_c, z_m = t_c * z_c, t_c * z_m + z_c * t_m + dot(z_m, gt)
    scale = lax.rsqrt(magnitude)
    a_c, a_m = z_c * scale, z_m * scale
    once = a_c * innovation + dot(a_m, dot(g, innovation))
    twice = a_c * once + dot(a_m, dot(g, once))
    v = dot(a_m, u) + twice[:, :1] * (1.0 / math.sqrt(members - 1))
    full = lax.dot_general(u, v, (((0,), (0,)), ((), ())), precision=highest, preferred_element_type=F32)
    diagonal = lax.broadcasted_iota(jnp.int32, (members, members), 0) == lax.broadcasted_iota(
        jnp.int32, (members, members), 1
    )
    full = full + jnp.where(diagonal, a_c, 0.0)
    column = jnp.sum(full, axis=0, keepdims=True)
    return full + (1.0 - column) * (1.0 / members)


def analyse_kernel(got_ref, gathered_ref, out_ref, coarse, fine, turned):
    sources, _, part, width = got_ref.shape
    members = sources * part
    columns, lines, inner, _ = out_ref.shape

    @pl.when(pl.program_id(0) == 0)
    def _():
        full = weights_of(gathered_ref[...], members)
        high = full.astype(BF16)
        coarse[...] = high
        fine[...] = (full - high.astype(F32)).astype(BF16)

    turn = (((0,), (0,)), ((), ()))
    for line in range(lines):
        states = got_ref[:, line].reshape(members, width)
        result = lax.dot_general(states, coarse[...], turn, preferred_element_type=F32)
        result += lax.dot_general(states, fine[...], turn, preferred_element_type=F32)
        for index in range(inner):
            rows = result[index * columns : (index + 1) * columns]
            for tile in range(members // LANES):
                turned[tile, pl.ds(line * inner + index, columns, stride=lines * inner), :] = rows[
                    :, tile * LANES : (tile + 1) * LANES
                ]
    for tile in range(members // LANES):
        out_ref[:, :, :, tile * LANES : (tile + 1) * LANES] = turned[tile].reshape(
            columns, lines, inner, LANES
        )


def analyse(got, gathered, columns, variables):
    sources, _, part, width = got.shape
    members = sources * part
    inner = width // columns
    return pl.pallas_call(
        analyse_kernel,
        out_shape=jax.ShapeDtypeStruct((columns, 2, variables, members), F32),
        grid=(variables // inner,),
        in_specs=[
            pl.BlockSpec((sources, 2, part, width), lambda i: (0, i, 0, 0)),
            pl.BlockSpec(gathered.shape, lambda i: (0, 0)),
        ],
        out_specs=pl.BlockSpec((columns, 2, inner, members), lambda i: (0, 0, i, 0)),
        scratch_shapes=[
            pltpu.VMEM((members, members), BF16),
            pltpu.VMEM((members, members), BF16),
            pltpu.VMEM((members // LANES, columns * 2 * inner, LANES), F32),
        ],
        compiler_params=pltpu.CompilerParams(vmem_limit_bytes=VMEM_LIMIT),
        name="analyse",
    )(got, gathered)


def on_device(
    prior_state,
    norm_scale,
    entry_kernel,
    closing_filter,
    observed_cell,
    observed_weight,
    observed_value,
    observed_precision,
):
    groups = lax.axis_size("mem")
    members, variables, lines, width = prior_state.shape
    hidden = entry_kernel.shape[1]
    columns = width // groups
    own = prior_state.reshape(members, variables * lines, width)
    gain = jnp.broadcast_to(jnp.repeat(norm_scale, lines)[:, None], (variables * lines, width))

    taps = entry_kernel.reshape(3, 3, hidden, variables)
    by_line = jnp.stack([jnp.pad(taps, ((j, 1 - j), (0, 0), (0, 0), (0, 0))) for j in range(2)])
    entry = by_line.reshape(2, 2, 2, 3, hidden, variables)
    entry = jnp.transpose(entry, (0, 4, 1, 3, 5, 2)).reshape(2 * hidden, 12 * variables)
    taps = closing_filter.reshape(3, 3, variables, hidden)
    by_line = jnp.stack([jnp.pad(taps, ((y, 1 - y), (0, 0), (0, 0), (0, 0))) for y in range(2)])
    closing = jnp.transpose(by_line, (2, 3, 0, 1, 4)).reshape(6 * variables, 4 * hidden)

    located = observed_cell[0, 0]
    observations = located.shape[0]
    cells = (located[:, None] == lax.iota(jnp.int32, columns * lines)[None, :]).astype(F32)
    cells = jnp.transpose(cells.reshape(observations, columns, lines), (2, 0, 1))
    weight = observed_weight[0, 0].reshape(observations, variables // groups, groups)
    operator = (
        jnp.transpose(weight, (1, 0, 2))[:, None, :, :, None] * cells[None, :, :, None, :]
    ).reshape(variables // groups * lines, observations, groups * columns)
    value = jnp.broadcast_to(observed_value[0, 0][:, None], (observations, LANES))
    precision = jnp.broadcast_to(observed_precision[0, 0][:, None], (observations, LANES))

    got = forecast(own, gain, entry, closing, groups)
    mine = observe(got, operator, value, precision)
    gathered = gather(mine, groups)
    gathered = gathered.reshape(groups * observations, mine.shape[1])
    return analyse(got, gathered, columns, variables)


def solution(mesh):
    return jax.shard_map(
        on_device,
        mesh=mesh,
        in_specs=(
            P("mem", None, "lat", None),
            P(),
            P(),
            P(),
            P("mem", "lat", None),
            P("mem", "lat", None, None),
            P("mem", "lat", None),
            P("mem", "lat", None),
        ),
        out_specs=P("mem", "lat", None, None),
        check_vma=False,
    )
```

```python
import functools
import math

import jax
import jax.numpy as jnp
from jax import lax
from jax.experimental import pallas as pl
from jax.experimental.pallas import tpu as pltpu
from jax.sharding import PartitionSpec as P

NS_ITERS = 3
LANES = 128
MESH = pl.DeviceIdType.MESH
VMEM_LIMIT = 56 * 1024 * 1024
F32 = jnp.float32
BF16 = jnp.bfloat16
highest = lax.Precision.HIGHEST


def forecast_kernel(
    own_ref, gain_ref, entry_ref, closing_ref, prior_ref, got_ref,
    below_ref, above_ref, parts_ref, stack, field,
    halo_send, halo_recv, part_send, part_recv, keep_sem,
):
    members, rows, width = own_ref.shape
    chunks = pl.num_programs(0)
    chunk_count = parts_ref.shape[0]
    chunk = pl.program_id(0)
    groups = lax.axis_size("mem")
    me = lax.axis_index("mem")
    band = lax.axis_index("lat")
    bands = lax.axis_size("lat")
    has_below = band > 0
    has_above = band < bands - 1

    def to_lower(index):
        piece = pl.ds(index * members, members)
        return pltpu.make_async_remote_copy(
            prior_ref.at[piece], above_ref.at[piece], halo_send.at[0, index], halo_recv.at[0, index],
            device_id={"lat": band - 1}, device_id_type=MESH,
        )

    def to_upper(index):
        piece = pl.ds(index * members, members)
        return pltpu.make_async_remote_copy(
            prior_ref.at[piece], below_ref.at[piece], halo_send.at[1, index], halo_recv.at[1, index],
            device_id={"lat": band + 1}, device_id_type=MESH,
        )

    def to_group(index, step):
        other = lax.rem(me + step, groups)
        return pltpu.make_async_remote_copy(
            parts_ref.at[index, other], got_ref.at[me, :, pl.ds(index * members, members)],
            part_send.at[index, step], part_recv.at[index, step],
            device_id={"mem": other}, device_id_type=MESH,
        )

    def to_self(index):
        return pltpu.make_async_copy(
            parts_ref.at[index, me], got_ref.at[me, :, pl.ds(index * members, members)],
            keep_sem.at[index],
        )

    @pl.when(chunk == 0)
    def _():
        barrier = pltpu.get_barrier_semaphore()
        for step in range(1, groups):
            pl.semaphore_signal(
                barrier, inc=1, device_id={"mem": lax.rem(me + step, groups)}, device_id_type=MESH
            )

        @pl.when(has_below)
        def _():
            pl.semaphore_signal(barrier, inc=1, device_id={"lat": band - 1}, device_id_type=MESH)

        @pl.when(has_above)
        def _():
            pl.semaphore_signal(barrier, inc=1, device_id={"lat": band + 1}, device_id_type=MESH)

        peers = jnp.where(has_below, 1, 0) + jnp.where(has_above, 1, 0)
        pl.semaphore_wait(barrier, groups - 1 + peers)
        for index in range(chunk_count):

            @pl.when(has_below)
            def _():
                to_lower(index).start()

            @pl.when(has_above)
            def _():
                to_upper(index).start()

    @pl.when(has_below)
    def _():
        to_upper(chunk).wait_recv()

    @pl.when(has_above)
    def _():
        to_lower(chunk).wait_recv()

    gain = gain_ref[...]
    half_below = jnp.where(has_below, 0.5, 0.0).astype(F32)
    half_above = jnp.where(has_above, 0.5, 0.0).astype(F32)

    def normed(values):
        values = values.astype(F32).reshape(rows // 8, 8, width)
        square = jnp.sum(values * values, axis=0)
        square = square + pltpu.roll(square, 2, 0)
        square = square + pltpu.roll(square, 4, 0)
        inverse = lax.rsqrt(square * (2.0 / rows) + 1e-06)
        return (values * inverse[None]).reshape(rows, width) * gain

    def gelu(value, half):
        inner = math.sqrt(2.0 / math.pi) * (value + 0.044715 * (value * value * value))
        return ((half * value) * (1.0 + jnp.tanh(inner))).astype(BF16)

    pair = 2
    slots = min(stack.shape[0], members // pair)
    half_rows = entry_ref.shape[0] // 2
    depth = entry_ref.shape[1] // 2

    def convolve(first, slot):
        for which in range(pair):
            lanes = slice(which * width, (which + 1) * width)
            member = first + which
            for block, (read, valid) in enumerate(
                (
                    (lambda: below_ref[chunk * members + member], has_below),
                    (lambda: own_ref[member], None),
                    (lambda: above_ref[chunk * members + member], has_above),
                )
            ):
                value = normed(read())
                if valid is not None:
                    value = jnp.where(valid, value, 0.0)
                for tap in range(3):
                    moved = value if tap == 1 else pltpu.roll(value, (1 - tap) % width, 1)
                    start = block * depth + tap * rows
                    stack[slot, start : start + rows, lanes] = moved.astype(BF16)
        entry = entry_ref[...]
        low = jnp.dot(entry, stack[slot, : 2 * depth, :], preferred_element_type=F32)
        high = jnp.dot(entry, stack[slot, depth:, :], preferred_element_type=F32)
        hidden = jnp.concatenate(
            [
                gelu(low[:half_rows], half_below),
                gelu(low[half_rows:], 0.5),
                gelu(high[:half_rows], 0.5),
                gelu(high[half_rows:], half_above),
            ],
            axis=0,
        )
        products = jnp.dot(closing_ref[...], hidden, preferred_element_type=F32)
        for which in range(pair):
            lanes = slice(which * width, (which + 1) * width)
            total = own_ref[first + which].astype(F32)
            for tap in range(3):
                part = products[tap * rows : (tap + 1) * rows, lanes]
                total = total + (part if tap == 1 else pltpu.roll(part, (1 - tap) % width, 1))
            field[pl.ds(pl.multiple_of((first + which) * rows, rows), rows), :] = total

    @pl.loop(0, members // (pair * slots))
    def _(turn):
        for slot in range(slots):
            convolve((turn * slots + slot) * pair, slot)

    columns = width // groups
    lane_group = lax.broadcasted_iota(jnp.int32, (members, width), 1) // columns

    @pl.loop(0, rows // (2 * groups))
    def _(piece):
        for line in range(2):
            tiles = [
                field[pl.ds(piece * (groups * 2) + (inner * 2 + line), members, stride=rows), :]
                for inner in range(groups)
            ]
            step = 1
            while step < groups:
                keep_low = (lane_group // step) % 2 == 0
                turned = list(tiles)
                for index in range(groups):
                    if (index // step) % 2 == 0:
                        a, b = tiles[index], tiles[index + step]
                        turned[index] = jnp.where(keep_low, a, pltpu.roll(b, step * columns, 1))
                        turned[index + step] = jnp.where(
                            keep_low, pltpu.roll(a, width - step * columns, 1), b
                        )
                tiles = turned
                step *= 2
            for group in range(groups):
                parts_ref[chunk, group, piece * 2 + line] = tiles[group].astype(BF16)

    for step in range(1, groups):
        to_group(chunk, step).start()
    to_self(chunk).start()

    @pl.when(chunk == chunks - 1)
    def _():
        for index in range(chunk_count):

            @pl.when(has_below)
            def _():
                to_lower(index).wait_send()

            @pl.when(has_above)
            def _():
                to_upper(index).wait_send()

            for step in range(1, groups):
                to_group(index, step).wait()
            to_self(index).wait()


def forecast(own, gain, entry, closing, groups):
    members, rows, width = own.shape
    chunk = min(16, members)
    chunks = members // chunk
    pieces = rows // groups
    whole = lambda a: pl.BlockSpec(a.shape, lambda i: (0,) * a.ndim)
    anywhere = pl.BlockSpec(memory_space=pl.ANY)
    return pl.pallas_call(
        forecast_kernel,
        out_shape=jax.ShapeDtypeStruct((groups, pieces, members, width), BF16),
        grid=(chunks,),
        in_specs=[
            pl.BlockSpec((chunk, rows, width), lambda i: (i, 0, 0)),
            whole(gain), whole(entry), whole(closing), anywhere,
        ],
        out_specs=anywhere,
        scratch_shapes=[
            pltpu.VMEM((members, rows, width), BF16),
            pltpu.VMEM((members, rows, width), BF16),
            pltpu.VMEM((chunks, groups, pieces, chunk, width), BF16),
            pltpu.VMEM((4, 9 * rows, 2 * width), BF16),
            pltpu.VMEM((chunk * rows, width), F32),
            pltpu.SemaphoreType.DMA((2, chunks)),
            pltpu.SemaphoreType.DMA((2, chunks)),
            pltpu.SemaphoreType.DMA((chunks, groups)),
            pltpu.SemaphoreType.DMA((chunks, groups)),
            pltpu.SemaphoreType.DMA((chunks,)),
        ],
        compiler_params=pltpu.CompilerParams(
            vmem_limit_bytes=VMEM_LIMIT, collective_id=0, has_side_effects=True
        ),
        name="forecast",
    )(own, gain, entry, closing, own)


def observe_kernel(
    got_ref, operator_ref, value_ref, precision_ref, all_ref, out_ref, send_sem, recv_sem, own_sem
):
    count = lax.axis_size("mem")
    me = lax.axis_index("mem")
    barrier = pltpu.get_barrier_semaphore()
    for step in range(1, count):
        pl.semaphore_signal(
            barrier, inc=1, device_id={"mem": lax.rem(me + step, count)}, device_id_type=MESH
        )
    sources, pieces, part, width = got_ref.shape
    observations = operator_ref.shape[1]
    total = None
    for piece in range(pieces):
        operator = operator_ref[piece]
        high = operator.astype(BF16)
        rest = operator - high.astype(F32)
        middle = rest.astype(BF16)
        low = (rest - middle.astype(F32)).astype(BF16)
        stacked = jnp.concatenate([high, middle, low], axis=0)
        states = got_ref[:, piece].reshape(sources * part, width)
        term = lax.dot_general(
            stacked, states, (((1,), (1,)), ((), ())), preferred_element_type=F32
        )
        total = term if total is None else total + term
    seen = total[:observations] + (total[observations : 2 * observations] + total[2 * observations :])
    mean = jnp.mean(seen, axis=1, keepdims=True)
    root = jnp.sqrt(precision_ref[...])
    out_ref[:, : sources * part] = (seen - mean) * root[:, :1]
    out_ref[:, sources * part :] = (value_ref[...] - mean) * root
    pl.semaphore_wait(barrier, count - 1)
    copies = []
    for step in range(1, count):
        copy = pltpu.make_async_remote_copy(
            out_ref, all_ref.at[me], send_sem.at[step], recv_sem.at[step],
            device_id={"mem": lax.rem(me + step, count)}, device_id_type=MESH,
        )
        copy.start()
        copies.append(copy)
    keep = pltpu.make_async_copy(out_ref, all_ref.at[me], own_sem)
    keep.start()
    keep.wait()
    for copy in copies:
        copy.wait()


def observe(got, operator, value, precision):
    sources, _, part, width = got.shape
    mine = (operator.shape[1], sources * part + LANES)
    return pl.pallas_call(
        observe_kernel,
        out_shape=jax.ShapeDtypeStruct((sources,) + mine, F32),
        scratch_shapes=[
            pltpu.VMEM(mine, F32),
            pltpu.SemaphoreType.DMA((sources,)),
            pltpu.SemaphoreType.DMA((sources,)),
            pltpu.SemaphoreType.DMA,
        ],
        compiler_params=pltpu.CompilerParams(
            vmem_limit_bytes=VMEM_LIMIT, collective_id=2, has_side_effects=True
        ),
        name="observe",
    )(got, operator, value, precision)


def weights_of(gathered, members):
    u = gathered[:, :members] * (1.0 / math.sqrt(members - 1))
    innovation = gathered[:, members:]
    count = u.shape[0]
    dot = functools.partial(jnp.dot, precision=highest, preferred_element_type=F32)
    g = lax.dot_general(u, u, (((1,), (1,)), ((), ())), precision=highest, preferred_element_type=F32)
    eye = (
        lax.broadcasted_iota(jnp.int32, (count, count), 0)
        == lax.broadcasted_iota(jnp.int32, (count, count), 1)
    ).astype(F32)
    total = lambda a: jnp.sum(jnp.sum(a, axis=1, keepdims=True), axis=0, keepdims=True)
    square = total(g * (g + 2.0 * eye)) + float(members)
    magnitude = jnp.sqrt(square)
    y_c, y_m = 1.0 / magnitude, eye / magnitude
    z_c, z_m = jnp.ones_like(magnitude), None
    for sweep in range(NS_ITERS):
        if z_m is None:
            p_m = y_m
        else:
            gy = dot(g, y_m)
            p_m = z_c * y_m + y_c * z_m + dot(z_m, gy)
        t_c, t_m = 0.5 * (3.0 - z_c * y_c), -0.5 * p_m
        gt = dot(g, t_m)
        if sweep + 1 < NS_ITERS:
            y_c, y_m = y_c * t_c, y_c * t_m + t_c * y_m + dot(y_m, gt)
        if z_m is None:
            z_c, z_m = t_c * z_c, z_c * t_m
        else:
            z_c, z_m = t_c * z_c, t_c * z_m + z_c * t_m + dot(z_m, gt)
    scale = lax.rsqrt(magnitude)
    a_c, a_m = z_c * scale, z_m * scale
    once = a_c * innovation + dot(a_m, dot(g, innovation))
    twice = a_c * once + dot(a_m, dot(g, once))
    v = dot(a_m, u) + twice[:, :1] * (1.0 / math.sqrt(members - 1))
    full = lax.dot_general(u, v, (((0,), (0,)), ((), ())), precision=highest, preferred_element_type=F32)
    diagonal = lax.broadcasted_iota(jnp.int32, (members, members), 0) == lax.broadcasted_iota(
        jnp.int32, (members, members), 1
    )
    full = full + jnp.where(diagonal, a_c, 0.0)
    column = jnp.sum(full, axis=0, keepdims=True)
    return full + (1.0 - column) * (1.0 / members)


def analyse_kernel(got_ref, gathered_ref, out_ref, coarse, fine, turned):
    sources, _, part, width = got_ref.shape
    members = sources * part
    columns, lines, inner, _ = out_ref.shape

    @pl.when(pl.program_id(0) == 0)
    def _():
        full = weights_of(gathered_ref[...], members)
        high = full.astype(BF16)
        coarse[...] = high
        fine[...] = (full - high.astype(F32)).astype(BF16)

    turn = (((0,), (0,)), ((), ()))
    for line in range(lines):
        states = got_ref[:, line].reshape(members, width)
        result = lax.dot_general(states, coarse[...], turn, preferred_element_type=F32)
        result += lax.dot_general(states, fine[...], turn, preferred_element_type=F32)
        for index in range(inner):
            rows = result[index * columns : (index + 1) * columns]
            for tile in range(members // LANES):
                turned[tile, pl.ds(line * inner + index, columns, stride=lines * inner), :] = rows[
                    :, tile * LANES : (tile + 1) * LANES
                ]
    for tile in range(members // LANES):
        out_ref[:, :, :, tile * LANES : (tile + 1) * LANES] = turned[tile].reshape(
            columns, lines, inner, LANES
        )


def analyse(got, gathered, columns, variables):
    sources, _, part, width = got.shape
    members = sources * part
    inner = width // columns
    return pl.pallas_call(
        analyse_kernel,
        out_shape=jax.ShapeDtypeStruct((columns, 2, variables, members), F32),
        grid=(variables // inner,),
        in_specs=[
            pl.BlockSpec((sources, 2, part, width), lambda i: (0, i, 0, 0)),
            pl.BlockSpec(gathered.shape, lambda i: (0, 0)),
        ],
        out_specs=pl.BlockSpec((columns, 2, inner, members), lambda i: (0, 0, i, 0)),
        scratch_shapes=[
            pltpu.VMEM((members, members), BF16),
            pltpu.VMEM((members, members), BF16),
            pltpu.VMEM((members // LANES, columns * 2 * inner, LANES), F32),
        ],
        compiler_params=pltpu.CompilerParams(vmem_limit_bytes=VMEM_LIMIT),
        name="analyse",
    )(got, gathered)


def on_device(
    prior_state,
    norm_scale,
    entry_kernel,
    closing_filter,
    observed_cell,
    observed_weight,
    observed_value,
    observed_precision,
):
    groups = lax.axis_size("mem")
    members, variables, lines, width = prior_state.shape
    hidden = entry_kernel.shape[1]
    columns = width // groups
    own = prior_state.reshape(members, variables * lines, width)
    gain = jnp.broadcast_to(jnp.repeat(norm_scale, lines)[:, None], (variables * lines, width))

    taps = entry_kernel.reshape(3, 3, hidden, variables)
    by_line = jnp.stack([jnp.pad(taps, ((j, 1 - j), (0, 0), (0, 0), (0, 0))) for j in range(2)])
    entry = by_line.reshape(2, 2, 2, 3, hidden, variables)
    entry = jnp.transpose(entry, (0, 4, 1, 3, 5, 2)).reshape(2 * hidden, 12 * variables)
    taps = closing_filter.reshape(3, 3, variables, hidden)
    by_line = jnp.stack([jnp.pad(taps, ((y, 1 - y), (0, 0), (0, 0), (0, 0))) for y in range(2)])
    closing = jnp.transpose(by_line, (2, 3, 0, 1, 4)).reshape(6 * variables, 4 * hidden)

    located = observed_cell[0, 0]
    observations = located.shape[0]
    cells = (located[:, None] == lax.iota(jnp.int32, columns * lines)[None, :]).astype(F32)
    cells = jnp.transpose(cells.reshape(observations, columns, lines), (2, 0, 1))
    weight = observed_weight[0, 0].reshape(observations, variables // groups, groups)
    operator = (
        jnp.transpose(weight, (1, 0, 2))[:, None, :, :, None] * cells[None, :, :, None, :]
    ).reshape(variables // groups * lines, observations, groups * columns)
    value = jnp.broadcast_to(observed_value[0, 0][:, None], (observations, LANES))
    precision = jnp.broadcast_to(observed_precision[0, 0][:, None], (observations, LANES))

    got = forecast(own, gain, entry, closing, groups)
    gathered = observe(got, operator, value, precision)
    gathered = gathered.reshape(groups * observations, gathered.shape[2])
    return analyse(got, gathered, columns, variables)


def solution(mesh):
    return jax.shard_map(
        on_device,
        mesh=mesh,
        in_specs=(
            P("mem", None, "lat", None),
            P(),
            P(),
            P(),
            P("mem", "lat", None),
            P("mem", "lat", None, None),
            P("mem", "lat", None),
            P("mem", "lat", None),
        ),
        out_specs=P("mem", "lat", None, None),
        check_vma=False,
    )
```
